32 devices in a mesh: grp: 8 (over z, core), swap: 4 (over y, x).
Axes of the slice: x: 2, y: 2, z: 4, core: 2. Of those that a mesh axis runs over, the one named last changes fastest.
Arguments:
- amplitudes: float32 [2, 8, 4, 4, 4, 8, 8, 128], P(None, 'grp', 'swap'), may hold values from -6 to 6
- low_gates: float32 [3, 2, 128, 128], replicated, may hold values from -0.375 to 0.375
- mid_gates: float32 [2, 2, 128, 128], replicated, may hold values from -0.375 to 0.375
- pair_gate: float32 [2, 2, 2], replicated, may hold values from -3 to 3
- slice_bits: int32 [13], replicated, may hold values from 0 to 1
- phase_angles: float32 [13, 128], replicated, may hold values from -3.140625 to 3.140625
Outputs:
- final_state: float32 [2, 8, 4, 4, 4, 8, 8, 128], P(None, 'grp', 'swap')
The draws below stay inside these ranges and needn't reach their ends.
All inputs are finite; a program needn't handle non-finite values.
Results may differ from the reference program's by a relative error of at most 0.00007.
Values sent between devices are 32-bit elements; how exact they have to be, the bound alone decides.
A program may use at most 64 MiB of HBM per device.

```python
import jax
import jax.numpy as jnp
from jax import lax

FIXED = 13
LOW = 128
TRADE = 16
MIDQ = 8
ROWS = 8
NG = 8
NS = 4
PB = 4


def plant(values, rng, low, top_value):
    spot = [jax.random.randint(jax.random.fold_in(rng, axis), (), 0, length) for axis, length in enumerate(values.shape)]
    longest = values.shape.index(max(values.shape))
    next_to = spot[:longest] + [(spot[longest] + 1) % values.shape[longest]] + spot[longest + 1:]
    return values.at[tuple(spot)].set(low).at[tuple(next_to)].set(top_value)


def block_scale(key, extent, shards, least, largest):
    def one(axis_at, shards_of):
        steps = jax.random.uniform(jax.random.fold_in(jax.random.fold_in(key, 6), axis_at), (shards_of,), jnp.float32, least / len(shards), largest / len(shards))
        return jnp.repeat(jnp.exp(steps), extent[axis_at] // shards_of).reshape((-1,) + (1,) * (len(extent) - axis_at - 1))

    factor_of = one(*shards[0])
    for cut in shards[1:]:
        factor_of = factor_of * one(*cut)
    return factor_of


def noise(key, extent, spread, reach, cuts=(), held_as=jnp.bfloat16):
    values = spread * jax.random.normal(key, extent, jnp.float32)
    if cuts:
        values = values * block_scale(key, extent, cuts, -0.22, 0.18)
    return jnp.clip(values, -reach, reach).astype(held_as)


def setup_inputs(seed: int = 0) -> dict:
    keys = jax.random.split(jax.random.key(seed), 7)
    amplitudes = noise(keys[0], (2, NG, NS, NS, PB, MIDQ, ROWS, LOW), 1.0, 6.0, ((1, 8), (2, 4)), jnp.float32)
    low_gates = noise(keys[1], (3, 2, LOW, LOW), (2 * LOW) ** -0.5, 0.375, (), jnp.float32)
    mid_gates = noise(keys[2], (2, 2, TRADE * MIDQ, TRADE * MIDQ), (2 * TRADE * MIDQ) ** -0.5, 0.375, (), jnp.float32)
    pair_gate = noise(keys[3], (2, 2, 2), 4 ** -0.5, 3.0, (), jnp.float32)
    slice_bits = plant(jax.random.randint(keys[4], (FIXED,), 0, 2), jax.random.fold_in(keys[4], 1), 0, 1).astype(jnp.int32)
    phase_angles = jnp.clip(jax.random.uniform(keys[5], (FIXED, LOW), jnp.float32, -3.140625, 3.140625), -3.140625, 3.140625)
    return {"amplitudes": amplitudes, "low_gates": low_gates, "mid_gates": mid_gates, "pair_gate": pair_gate, "slice_bits": slice_bits, "phase_angles": phase_angles}


highest = lax.Precision.HIGHEST


def low_gate(psi, matrix):
    real_part = jnp.einsum("...k,ik->...i", psi[0], matrix[0], precision=highest, preferred_element_type=jnp.float32) - jnp.einsum("...k,ik->...i", psi[1], matrix[1], precision=highest, preferred_element_type=jnp.float32)
    imag_part = jnp.einsum("...k,ik->...i", psi[1], matrix[0], precision=highest, preferred_element_type=jnp.float32) + jnp.einsum("...k,ik->...i", psi[0], matrix[1], precision=highest, preferred_element_type=jnp.float32)
    return jnp.stack([real_part, imag_part])


def mid_gate(psi, matrix):
    shape_now = psi.shape
    order = matrix.shape[1]
    flat = psi.reshape(2, -1, order, shape_now[-2] * shape_now[-1])
    real_part = jnp.einsum("ik,bkm->bim", matrix[0], flat[0], precision=highest, preferred_element_type=jnp.float32) - jnp.einsum("ik,bkm->bim", matrix[1], flat[1], precision=highest, preferred_element_type=jnp.float32)
    imag_part = jnp.einsum("ik,bkm->bim", matrix[0], flat[1], precision=highest, preferred_element_type=jnp.float32) + jnp.einsum("ik,bkm->bim", matrix[1], flat[0], precision=highest, preferred_element_type=jnp.float32)
    return jnp.stack([real_part, imag_part]).reshape(shape_now)


def reference(amplitudes, low_gates, mid_gates, pair_gate, slice_bits, phase_angles):
    theta = jnp.dot(slice_bits.astype(jnp.float32), phase_angles, precision=highest, preferred_element_type=jnp.float32)
    cosine = jnp.cos(theta)
    sine = jnp.sin(theta)
    phased = jnp.stack([amplitudes[0] * cosine - amplitudes[1] * sine, amplitudes[0] * sine + amplitudes[1] * cosine])
    first = low_gate(phased, low_gates[0])
    second = mid_gate(first, mid_gates[0])
    third = low_gate(second, low_gates[1])
    outer = third.shape[1]
    halves = third.reshape((2, 2, outer // 2) + third.shape[2:])
    lower = halves[:, 0]
    upper = halves[:, 1]

    def pair_row(target):
        real_part = (pair_gate[0, target, 0] * lower[0] - pair_gate[1, target, 0] * lower[1]) + (pair_gate[0, target, 1] * upper[0] - pair_gate[1, target, 1] * upper[1])
        imag_part = (pair_gate[0, target, 0] * lower[1] + pair_gate[1, target, 0] * lower[0]) + (pair_gate[0, target, 1] * upper[1] + pair_gate[1, target, 1] * upper[0])
        return jnp.stack([real_part, imag_part])

    paired = jnp.stack([pair_row(0), pair_row(1)], axis=1).reshape(third.shape)
    traded = jnp.swapaxes(paired, 2, 3)
    fourth = mid_gate(traded, mid_gates[1])
    return low_gate(fourth, low_gates[2])
```

```python
import functools

import jax
import jax.numpy as jnp
from jax import lax
from jax.experimental import pallas as pl
from jax.experimental.pallas import tpu as pltpu
from jax.sharding import PartitionSpec as P

MESH = pl.DeviceIdType.MESH
highest = lax.Precision.HIGHEST


def dot(a, b):
    return jnp.dot(a, b, precision=highest, preferred_element_type=jnp.float32)


def dot_nt(a, b):
    return lax.dot_general(
        a, b, (((1,), (1,)), ((), ())), precision=highest, preferred_element_type=jnp.float32
    )


def embedded(re, im):
    return jnp.concatenate(
        [jnp.concatenate([re, -im], axis=1), jnp.concatenate([im, re], axis=1)], axis=0
    )


def mixed(own, other, own_re, own_im, other_re, other_im):
    re = (own[0] * own_re - own[1] * own_im) + (other[0] * other_re - other[1] * other_im)
    im = (own[0] * own_im + own[1] * own_re) + (other[0] * other_im + other[1] * other_re)
    return re, im


def kernel(
    dims,
    x_ref, low_ref, mid_ref, pair_ref, bits_ref, angle_ref,
    out_ref,
    x_v, low_v, mid_v, angle_v, out_v,
    early_x, early_rx, early_y, early_t, late_y, late_t, late_z, late_rz,
    load_sem, ze_send, ze_recv, zl_send, zl_recv, ae_send, ae_recv, al_send, al_recv, store_sem,
):
    groups, swaps, m_size, rows, low, early, blocks = dims
    late = rows - early
    part = m_size // swaps
    piece = m_size // blocks
    grp = lax.axis_index("grp")
    me = lax.axis_index("swap")
    half = groups // 2
    top = grp // half
    partner = (grp + half) % groups

    barrier = pltpu.get_barrier_semaphore()
    pl.semaphore_signal(barrier, inc=1, device_id={"grp": partner}, device_id_type=MESH)
    for d in range(1, swaps):
        pl.semaphore_signal(
            barrier, inc=1, device_id={"swap": lax.bitwise_xor(me, d)}, device_id_type=MESH
        )
    loads = [
        pltpu.make_async_copy(src, dst, load_sem.at[i])
        for i, (src, dst) in enumerate(
            [(x_ref, x_v), (low_ref, low_v), (mid_ref, mid_v), (angle_ref, angle_v)]
        )
    ]
    for load in loads:
        load.start()
    loads[0].wait()

    def x_row(c, r):
        return x_v[pl.ds(c * m_size * rows + r, m_size, stride=rows), :]

    for r in range(early):
        for c in range(2):
            early_x[r, c] = x_row(c, r)
    pl.semaphore_wait(barrier, swaps)

    raw = [
        pltpu.make_async_remote_copy(
            src_ref=early_x.at[r], dst_ref=early_rx.at[r],
            send_sem=ze_send.at[r], recv_sem=ze_recv.at[r],
            device_id={"grp": partner}, device_id_type=MESH,
        )
        for r in range(early)
    ]
    for copy in raw:
        copy.start()

    for load in loads[1:]:
        load.wait()
    theta = bits_ref[0].astype(jnp.float32) * angle_v[0:1, :]
    for j in range(1, angle_v.shape[0]):
        theta = theta + bits_ref[j].astype(jnp.float32) * angle_v[j : j + 1, :]
    cosine, sine = jnp.cos(theta), jnp.sin(theta)
    w = jnp.concatenate([low_v[0, 0], low_v[0, 1]], axis=0)
    for i in range(1, low_v.shape[0]):
        w = dot(embedded(low_v[i, 0], low_v[i, 1]), w)
    w_re, w_im = w[:low], w[low:]
    w = embedded(w_re * cosine - w_im * sine, w_re * sine + w_im * cosine)
    mid_first = embedded(mid_v[0, 0], mid_v[0, 1])
    mid_second = embedded(mid_v[1, 0], mid_v[1, 1])

    def first_gates(pairs, y_ref):
        for i, (re, im) in enumerate(pairs):
            y = dot_nt(jnp.concatenate([re, im], axis=1), w)
            y = dot(mid_first, jnp.concatenate([y[:, :low], y[:, low:]], axis=0))
            y_ref[i, 0] = y[:m_size]
            y_ref[i, 1] = y[m_size:]

    def trade(y_ref, t_ref, send, recv):
        mine = pl.ds(pl.multiple_of(me * part, part), part)
        copies = []
        for d in range(1, swaps):
            to = lax.bitwise_xor(me, d)
            copy = pltpu.make_async_remote_copy(
                src_ref=y_ref.at[:, :, pl.ds(pl.multiple_of(to * part, part), part), :],
                dst_ref=t_ref.at[:, :, mine, :],
                send_sem=send.at[d], recv_sem=recv.at[d],
                device_id={"swap": to}, device_id_type=MESH,
            )
            copy.start()
            copies.append(copy)
        t_ref[:, :, mine, :] = y_ref[:, :, mine, :]
        for copy in copies:
            copy.wait()

    def last_gate(t_ref, i):
        z = dot(mid_second, jnp.concatenate([t_ref[i, 0], t_ref[i, 1]], axis=0))
        return z[:m_size], z[m_size:]

    own_re, own_im = pair_ref[0, top, top], pair_ref[1, top, top]
    other_re, other_im = pair_ref[0, top, 1 - top], pair_ref[1, top, 1 - top]

    first_gates([(x_row(0, r), x_row(1, r)) for r in range(early, rows)], late_y)
    trade(late_y, late_t, al_send, al_recv)
    for i in range(late):
        z_re, z_im = last_gate(late_t, i)
        late_z[i, 0] = z_re
        late_z[i, 1] = z_im
    finished = []
    for k in range(blocks):
        rows_k = pl.ds(k * piece, piece)
        copy = pltpu.make_async_remote_copy(
            src_ref=late_z.at[:, :, rows_k, :], dst_ref=late_rz.at[:, :, rows_k, :],
            send_sem=zl_send.at[k], recv_sem=zl_recv.at[k],
            device_id={"grp": partner}, device_id_type=MESH,
        )
        copy.start()
        finished.append(copy)

    for copy in raw:
        copy.wait()
    first_gates(
        [
            mixed(
                (early_x[r, 0], early_x[r, 1]), (early_rx[r, 0], early_rx[r, 1]),
                own_re, own_im, other_re, other_im,
            )
            for r in range(early)
        ],
        early_y,
    )
    trade(early_y, early_t, ae_send, ae_recv)
    for r in range(early):
        for c, value in enumerate(last_gate(early_t, r)):
            out_v[pl.ds(c * m_size * rows + r, m_size, stride=rows), :] = value

    stores = []
    for k in range(blocks):
        finished[k].wait_recv()
        at = slice(k * piece, (k + 1) * piece)
        for i in range(late):
            pair = mixed(
                (late_z[i, 0, at], late_z[i, 1, at]), (late_rz[i, 0, at], late_rz[i, 1, at]),
                own_re, own_im, other_re, other_im,
            )
            for c in range(2):
                start = (c * m_size + k * piece) * rows + early + i
                out_v[pl.ds(start, piece, stride=rows), :] = pair[c]
        for c in range(2):
            span = pl.ds((c * m_size + k * piece) * rows, piece * rows)
            store = pltpu.make_async_copy(out_v.at[span], out_ref.at[span], store_sem.at[2 * k + c])
            store.start()
            stores.append(store)
    for copy in finished:
        copy.wait_send()
    for store in stores:
        store.wait()


def local(groups, swaps, amplitudes, low_gates, mid_gates, pair_gate, slice_bits, phase_angles):
    _, _, _, a_size, b_size, q_size, rows, low = amplitudes.shape
    m_size = a_size * b_size * q_size
    early = max(1, rows * 3 // 8)
    late = rows - early
    blocks = 8
    flat = amplitudes.reshape(2 * m_size * rows, low)
    f32 = jnp.float32
    dma = pltpu.SemaphoreType.DMA
    anywhere = pl.BlockSpec(memory_space=pl.ANY)
    scalars = pl.BlockSpec(memory_space=pltpu.SMEM)
    out = pl.pallas_call(
        functools.partial(kernel, (groups, swaps, m_size, rows, low, early, blocks)),
        out_shape=jax.ShapeDtypeStruct(flat.shape, f32),
        in_specs=[anywhere, anywhere, anywhere, scalars, scalars, anywhere],
        out_specs=anywhere,
        scratch_shapes=[
            pltpu.VMEM(flat.shape, f32),
            pltpu.VMEM(low_gates.shape, f32),
            pltpu.VMEM(mid_gates.shape, f32),
            pltpu.VMEM(phase_angles.shape, f32),
            pltpu.VMEM(flat.shape, f32),
        ]
        + [pltpu.VMEM((early, 2, m_size, low), f32)] * 4
        + [pltpu.VMEM((late, 2, m_size, low), f32)] * 4
        + [
            dma((4,)),
            dma((early,)), dma((early,)),
            dma((blocks,)), dma((blocks,)),
            dma((swaps,)), dma((swaps,)), dma((swaps,)), dma((swaps,)),
            dma((2 * blocks,)),
        ],
        compiler_params=pltpu.CompilerParams(collective_id=0, has_side_effects=True),
        name="evolve",
    )(flat, low_gates, mid_gates, pair_gate, slice_bits, phase_angles)
    return out.reshape(amplitudes.shape)


def solution(mesh):
    spec = P(None, "grp", "swap", None, None, None, None, None)
    return jax.shard_map(
        functools.partial(local, mesh.shape["grp"], mesh.shape["swap"]),
        mesh=mesh,
        in_specs=(spec, P(), P(), P(), P(), P()),
        out_specs=spec,
        check_vma=False,
    )
```

```python
import functools

import jax
import jax.numpy as jnp
from jax import lax
from jax.experimental import pallas as pl
from jax.experimental.pallas import tpu as pltpu
from jax.sharding import PartitionSpec as P

MESH = pl.DeviceIdType.MESH
highest = lax.Precision.HIGHEST


def dot(a, b):
    return jnp.dot(a, b, precision=highest, preferred_element_type=jnp.float32)


def dot_nt(a, b):
    return lax.dot_general(
        a, b, (((1,), (1,)), ((), ())), precision=highest, preferred_element_type=jnp.float32
    )


def embedded(re, im):
    return jnp.concatenate(
        [jnp.concatenate([re, -im], axis=1), jnp.concatenate([im, re], axis=1)], axis=0
    )


def mixed(own, other, own_re, own_im, other_re, other_im):
    re = (own[0] * own_re - own[1] * own_im) + (other[0] * other_re - other[1] * other_im)
    im = (own[0] * own_im + own[1] * own_re) + (other[0] * other_im + other[1] * other_re)
    return re, im


def kernel(
    dims,
    x_ref, low_ref, mid_ref, pair_ref, bits_ref, angle_ref,
    out_ref,
    x_v, low_v, mid_v, angle_v, out_v,
    early_x, early_rx, early_y, early_t, late_y, late_t, late_z, late_rz,
    load_sem, ze_send, ze_recv, zl_send, zl_recv, ae_send, ae_recv, al_send, al_recv, store_sem, gate_sem,
):
    groups, swaps, m_size, rows, low, early, blocks = dims
    late = rows - early
    part = m_size // swaps
    piece = m_size // blocks
    grp = lax.axis_index("grp")
    me = lax.axis_index("swap")
    half = groups // 2
    top = grp // half
    partner = (grp + half) % groups
    quarter = half // 2
    gated = quarter > 0
    if gated:
        outer = (grp % half) // quarter
        mate = grp + quarter - 2 * quarter * outer
        holds = jnp.logical_and(top == 1, outer == 1)
        frees = jnp.logical_and(top == 1, outer == 0)

    barrier = pltpu.get_barrier_semaphore()
    pl.semaphore_signal(barrier, inc=1, device_id={"grp": partner}, device_id_type=MESH)
    if gated:
        pl.semaphore_signal(barrier, inc=1, device_id={"grp": mate}, device_id_type=MESH)
    for d in range(1, swaps):
        pl.semaphore_signal(
            barrier, inc=1, device_id={"swap": lax.bitwise_xor(me, d)}, device_id_type=MESH
        )
    loads = [
        pltpu.make_async_copy(src, dst, load_sem.at[i])
        for i, (src, dst) in enumerate(
            [(x_ref, x_v), (low_ref, low_v), (mid_ref, mid_v), (angle_ref, angle_v)]
        )
    ]
    for load in loads:
        load.start()
    loads[0].wait()

    def x_row(c, r):
        return x_v[pl.ds(c * m_size * rows + r, m_size, stride=rows), :]

    for r in range(early):
        for c in range(2):
            early_x[r, c] = x_row(c, r)
    pl.semaphore_wait(barrier, swaps + 1 if gated else swaps)

    raw = [
        pltpu.make_async_remote_copy(
            src_ref=early_x.at[r], dst_ref=early_rx.at[r],
            send_sem=ze_send.at[r], recv_sem=ze_recv.at[r],
            device_id={"grp": partner}, device_id_type=MESH,
        )
        for r in range(early)
    ]
    for copy in raw:
        copy.start()

    for load in loads[1:]:
        load.wait()
    theta = bits_ref[0].astype(jnp.float32) * angle_v[0:1, :]
    for j in range(1, angle_v.shape[0]):
        theta = theta + bits_ref[j].astype(jnp.float32) * angle_v[j : j + 1, :]
    cosine, sine = jnp.cos(theta), jnp.sin(theta)
    w = jnp.concatenate([low_v[0, 0], low_v[0, 1]], axis=0)
    for i in range(1, low_v.shape[0]):
        w = dot(embedded(low_v[i, 0], low_v[i, 1]), w)
    w_re, w_im = w[:low], w[low:]
    w = embedded(w_re * cosine - w_im * sine, w_re * sine + w_im * cosine)
    mid_first = embedded(mid_v[0, 0], mid_v[0, 1])
    mid_second = embedded(mid_v[1, 0], mid_v[1, 1])

    def first_gates(pairs, y_ref):
        for i, (re, im) in enumerate(pairs):
            y = dot_nt(jnp.concatenate([re, im], axis=1), w)
            y = dot(mid_first, jnp.concatenate([y[:, :low], y[:, low:]], axis=0))
            y_ref[i, 0] = y[:m_size]
            y_ref[i, 1] = y[m_size:]

    def trade(y_ref, t_ref, send, recv):
        mine = pl.ds(pl.multiple_of(me * part, part), part)
        copies = []
        for d in range(1, swaps):
            to = lax.bitwise_xor(me, d)
            copy = pltpu.make_async_remote_copy(
                src_ref=y_ref.at[:, :, pl.ds(pl.multiple_of(to * part, part), part), :],
                dst_ref=t_ref.at[:, :, mine, :],
                send_sem=send.at[d], recv_sem=recv.at[d],
                device_id={"swap": to}, device_id_type=MESH,
            )
            copy.start()
            copies.append(copy)
        t_ref[:, :, mine, :] = y_ref[:, :, mine, :]
        for copy in copies:
            copy.wait()

    def last_gate(t_ref, i):
        z = dot(mid_second, jnp.concatenate([t_ref[i, 0], t_ref[i, 1]], axis=0))
        return z[:m_size], z[m_size:]

    own_re, own_im = pair_ref[0, top, top], pair_ref[1, top, top]
    other_re, other_im = pair_ref[0, top, 1 - top], pair_ref[1, top, 1 - top]

    first_gates([(x_row(0, r), x_row(1, r)) for r in range(early, rows)], late_y)
    trade(late_y, late_t, al_send, al_recv)
    for i in range(late):
        z_re, z_im = last_gate(late_t, i)
        late_z[i, 0] = z_re
        late_z[i, 1] = z_im
    finished = []
    for k in range(blocks):
        rows_k = pl.ds(k * piece, piece)
        copy = pltpu.make_async_remote_copy(
            src_ref=late_z.at[:, :, rows_k, :], dst_ref=late_rz.at[:, :, rows_k, :],
            send_sem=zl_send.at[k], recv_sem=zl_recv.at[k],
            device_id={"grp": partner}, device_id_type=MESH,
        )
        if gated and k == blocks - 1:
            pl.when(jnp.logical_not(holds))(copy.start)
        else:
            copy.start()
        finished.append(copy)

    for copy in raw:
        copy.wait()
    first_gates(
        [
            mixed(
                (early_x[r, 0], early_x[r, 1]), (early_rx[r, 0], early_rx[r, 1]),
                own_re, own_im, other_re, other_im,
            )
            for r in range(early)
        ],
        early_y,
    )
    trade(early_y, early_t, ae_send, ae_recv)
    for r in range(early):
        for c, value in enumerate(last_gate(early_t, r)):
            out_v[pl.ds(c * m_size * rows + r, m_size, stride=rows), :] = value

    stores = []
    for k in range(blocks):
        finished[k].wait_recv()
        at = slice(k * piece, (k + 1) * piece)
        for i in range(late):
            pair = mixed(
                (late_z[i, 0, at], late_z[i, 1, at]), (late_rz[i, 0, at], late_rz[i, 1, at]),
                own_re, own_im, other_re, other_im,
            )
            for c in range(2):
                start = (c * m_size + k * piece) * rows + early + i
                out_v[pl.ds(start, piece, stride=rows), :] = pair[c]
        for c in range(2):
            span = pl.ds((c * m_size + k * piece) * rows, piece * rows)
            store = pltpu.make_async_copy(out_v.at[span], out_ref.at[span], store_sem.at[2 * k + c])
            store.start()
            stores.append(store)
        if gated and k == blocks - 3:
            finished[blocks - 2].wait_send()

            @pl.when(frees)
            def _():
                pl.semaphore_signal(gate_sem, inc=1, device_id={"grp": mate}, device_id_type=MESH)

            @pl.when(holds)
            def _():
                pl.semaphore_wait(gate_sem, 1)
                finished[blocks - 1].start()
    for k in range(blocks):
        if not gated or k != blocks - 2:
            finished[k].wait_send()
    for store in stores:
        store.wait()


def local(groups, swaps, amplitudes, low_gates, mid_gates, pair_gate, slice_bits, phase_angles):
    _, _, _, a_size, b_size, q_size, rows, low = amplitudes.shape
    m_size = a_size * b_size * q_size
    early = max(1, rows * 3 // 8)
    late = rows - early
    blocks = 8
    flat = amplitudes.reshape(2 * m_size * rows, low)
    f32 = jnp.float32
    dma = pltpu.SemaphoreType.DMA
    anywhere = pl.BlockSpec(memory_space=pl.ANY)
    scalars = pl.BlockSpec(memory_space=pltpu.SMEM)
    out = pl.pallas_call(
        functools.partial(kernel, (groups, swaps, m_size, rows, low, early, blocks)),
        out_shape=jax.ShapeDtypeStruct(flat.shape, f32),
        in_specs=[anywhere, anywhere, anywhere, scalars, scalars, anywhere],
        out_specs=anywhere,
        scratch_shapes=[
            pltpu.VMEM(flat.shape, f32),
            pltpu.VMEM(low_gates.shape, f32),
            pltpu.VMEM(mid_gates.shape, f32),
            pltpu.VMEM(phase_angles.shape, f32),
            pltpu.VMEM(flat.shape, f32),
        ]
        + [pltpu.VMEM((early, 2, m_size, low), f32)] * 4
        + [pltpu.VMEM((late, 2, m_size, low), f32)] * 4
        + [
            dma((4,)),
            dma((early,)), dma((early,)),
            dma((blocks,)), dma((blocks,)),
            dma((swaps,)), dma((swaps,)), dma((swaps,)), dma((swaps,)),
            dma((2 * blocks,)),
            pltpu.SemaphoreType.REGULAR,
        ],
        compiler_params=pltpu.CompilerParams(collective_id=0, has_side_effects=True),
        name="evolve",
    )(flat, low_gates, mid_gates, pair_gate, slice_bits, phase_angles)
    return out.reshape(amplitudes.shape)


def solution(mesh):
    spec = P(None, "grp", "swap", None, None, None, None, None)
    return jax.shard_map(
        functools.partial(local, mesh.shape["grp"], mesh.shape["swap"]),
        mesh=mesh,
        in_specs=(spec, P(), P(), P(), P(), P()),
        out_specs=spec,
        check_vma=False,
    )
```

```python
import functools

import jax
import jax.numpy as jnp
from jax import lax
from jax.experimental import pallas as pl
from jax.experimental.pallas import tpu as pltpu
from jax.sharding import PartitionSpec as P

MESH = pl.DeviceIdType.MESH
highest = lax.Precision.HIGHEST


def dot(a, b):
    return jnp.dot(a, b, precision=highest, preferred_element_type=jnp.float32)


def dot_nt(a, b):
    return lax.dot_general(
        a, b, (((1,), (1,)), ((), ())), precision=highest, preferred_element_type=jnp.float32
    )


def embedded(re, im):
    return jnp.concatenate(
        [jnp.concatenate([re, -im], axis=1), jnp.concatenate([im, re], axis=1)], axis=0
    )


def mixed(own, other, own_re, own_im, other_re, other_im):
    re = (own[0] * own_re - own[1] * own_im) + (other[0] * other_re - other[1] * other_im)
    im = (own[0] * own_im + own[1] * own_re) + (other[0] * other_im + other[1] * other_re)
    return re, im


def kernel(
    dims,
    x_ref, low_ref, mid_ref, pair_in, bits_in, angle_ref,
    out_ref,
    x_v, low_v, mid_v, angle_v, pair_ref, bits_ref, out_v,
    early_x, early_rx, early_y, early_t, late_y, late_t, late_z, late_rz,
    x_sem, load_sem, ze_send, ze_recv, zl_send, zl_recv, ae_send, ae_recv, al_send, al_recv, store_sem,
):
    groups, swaps, m_size, rows, low, early, blocks, pieces = dims
    late = rows - early
    part = m_size // swaps
    piece = m_size // blocks
    grp = lax.axis_index("grp")
    me = lax.axis_index("swap")
    half = groups // 2
    top = grp // half
    partner = (grp + half) % groups
    holds = 4 * grp >= 3 * groups

    barrier = pltpu.get_barrier_semaphore()
    pl.semaphore_signal(barrier, inc=1, device_id={"grp": partner}, device_id_type=MESH)
    for d in range(1, swaps):
        pl.semaphore_signal(
            barrier, inc=1, device_id={"swap": lax.bitwise_xor(me, d)}, device_id_type=MESH
        )
    span = m_size // pieces
    x_loads = []
    for j in range(pieces):
        for c in range(2):
            at = pl.ds((c * m_size + j * span) * rows, span * rows)
            x_loads.append(
                pltpu.make_async_copy(x_ref.at[at], x_v.at[at], x_sem.at[2 * j + c])
            )
    loads = [
        pltpu.make_async_copy(src, dst, load_sem.at[i])
        for i, (src, dst) in enumerate([(low_ref, low_v), (mid_ref, mid_v), (angle_ref, angle_v), (pair_in, pair_ref), (bits_in, bits_ref)])
    ]
    for load in x_loads + loads:
        load.start()

    def x_row(c, r):
        return x_v[pl.ds(c * m_size * rows + r, m_size, stride=rows), :]

    def gather(j):
        for c in range(2):
            x_loads[2 * j + c].wait()
        for r in range(early):
            for c in range(2):
                start = (c * m_size + j * span) * rows + r
                early_x[r, c, j * span : (j + 1) * span, :] = x_v[pl.ds(start, span, stride=rows), :]

    raw = []
    for j in range(pieces):
        at = pl.ds(j * span, span)
        raw.append(
            pltpu.make_async_remote_copy(
                src_ref=early_x.at[:, :, at, :], dst_ref=early_rx.at[:, :, at, :],
                send_sem=ze_send.at[j], recv_sem=ze_recv.at[j],
                device_id={"grp": partner}, device_id_type=MESH,
            )
        )
    gather(0)
    gather(1)
    pl.semaphore_wait(barrier, swaps)
    for j in range(pieces):
        raw[j].start()
        if j + 2 < pieces:
            gather(j + 2)

    for load in loads:
        load.wait()
    theta = bits_ref[0].astype(jnp.float32) * angle_v[0:1, :]
    for j in range(1, angle_v.shape[0]):
        theta = theta + bits_ref[j].astype(jnp.float32) * angle_v[j : j + 1, :]
    cosine, sine = jnp.cos(theta), jnp.sin(theta)
    w = jnp.concatenate([low_v[0, 0], low_v[0, 1]], axis=0)
    for i in range(1, low_v.shape[0]):
        w = dot(embedded(low_v[i, 0], low_v[i, 1]), w)
    w_re, w_im = w[:low], w[low:]
    w = embedded(w_re * cosine - w_im * sine, w_re * sine + w_im * cosine)
    mid_first = embedded(mid_v[0, 0], mid_v[0, 1])
    mid_second = embedded(mid_v[1, 0], mid_v[1, 1])

    def first_gates(pairs, y_ref):
        for i, (re, im) in enumerate(pairs):
            y = dot_nt(jnp.concatenate([re, im], axis=1), w)
            y = dot(mid_first, jnp.concatenate([y[:, :low], y[:, low:]], axis=0))
            y_ref[i, 0] = y[:m_size]
            y_ref[i, 1] = y[m_size:]

    def trade(y_ref, t_ref, send, recv):
        mine = pl.ds(pl.multiple_of(me * part, part), part)
        copies = []
        for d in range(1, swaps):
            to = lax.bitwise_xor(me, d)
            copy = pltpu.make_async_remote_copy(
                src_ref=y_ref.at[:, :, pl.ds(pl.multiple_of(to * part, part), part), :],
                dst_ref=t_ref.at[:, :, mine, :],
                send_sem=send.at[d], recv_sem=recv.at[d],
                device_id={"swap": to}, device_id_type=MESH,
            )
            copy.start()
            copies.append(copy)
        t_ref[:, :, mine, :] = y_ref[:, :, mine, :]
        for copy in copies:
            copy.wait()

    def last_gate(t_ref, i):
        z = dot(mid_second, jnp.concatenate([t_ref[i, 0], t_ref[i, 1]], axis=0))
        return z[:m_size], z[m_size:]

    own_re, own_im = pair_ref[0, top, top], pair_ref[1, top, top]
    other_re, other_im = pair_ref[0, top, 1 - top], pair_ref[1, top, 1 - top]

    first_gates([(x_row(0, r), x_row(1, r)) for r in range(early, rows)], late_y)
    trade(late_y, late_t, al_send, al_recv)
    for i in range(late):
        z_re, z_im = last_gate(late_t, i)
        late_z[i, 0] = z_re
        late_z[i, 1] = z_im
    finished = []
    for k in range(blocks):
        rows_k = pl.ds(k * piece, piece)
        copy = pltpu.make_async_remote_copy(
            src_ref=late_z.at[:, :, rows_k, :], dst_ref=late_rz.at[:, :, rows_k, :],
            send_sem=zl_send.at[k], recv_sem=zl_recv.at[k],
            device_id={"grp": partner}, device_id_type=MESH,
        )
        if k == blocks - 1:
            pl.when(jnp.logical_not(holds))(copy.start)
        else:
            copy.start()
        finished.append(copy)

    for copy in raw:
        copy.wait()
    first_gates(
        [
            mixed(
                (early_x[r, 0], early_x[r, 1]), (early_rx[r, 0], early_rx[r, 1]),
                own_re, own_im, other_re, other_im,
            )
            for r in range(early)
        ],
        early_y,
    )
    trade(early_y, early_t, ae_send, ae_recv)
    for r in range(early):
        for c, value in enumerate(last_gate(early_t, r)):
            out_v[pl.ds(c * m_size * rows + r, m_size, stride=rows), :] = value

    stores = []
    for k in range(blocks):
        finished[k].wait_recv()
        at = slice(k * piece, (k + 1) * piece)
        for i in range(late):
            pair = mixed(
                (late_z[i, 0, at], late_z[i, 1, at]), (late_rz[i, 0, at], late_rz[i, 1, at]),
                own_re, own_im, other_re, other_im,
            )
            for c in range(2):
                start = (c * m_size + k * piece) * rows + early + i
                out_v[pl.ds(start, piece, stride=rows), :] = pair[c]
        for c in range(2):
            span = pl.ds((c * m_size + k * piece) * rows, piece * rows)
            store = pltpu.make_async_copy(out_v.at[span], out_ref.at[span], store_sem.at[2 * k + c])
            store.start()
            stores.append(store)
        if k == blocks - 3:
            pl.when(holds)(finished[blocks - 1].start)
    for copy in finished:
        copy.wait_send()
    for store in stores:
        store.wait()


def local(groups, swaps, amplitudes, low_gates, mid_gates, pair_gate, slice_bits, phase_angles):
    _, _, _, a_size, b_size, q_size, rows, low = amplitudes.shape
    m_size = a_size * b_size * q_size
    early = max(1, rows * 3 // 8)
    late = rows - early
    blocks, pieces = 8, 4
    flat = amplitudes.reshape(2 * m_size * rows, low)
    f32 = jnp.float32
    dma = pltpu.SemaphoreType.DMA
    anywhere = pl.BlockSpec(memory_space=pl.ANY)
    in_hbm = [
        pltpu.with_memory_space_constraint(value, pltpu.HBM)
        for value in (flat, low_gates, mid_gates, pair_gate, slice_bits, phase_angles)
    ]
    out = pl.pallas_call(
        functools.partial(kernel, (groups, swaps, m_size, rows, low, early, blocks, pieces)),
        out_shape=jax.ShapeDtypeStruct(flat.shape, f32),
        in_specs=[anywhere] * 6,
        out_specs=anywhere,
        scratch_shapes=[
            pltpu.VMEM(flat.shape, f32),
            pltpu.VMEM(low_gates.shape, f32),
            pltpu.VMEM(mid_gates.shape, f32),
            pltpu.VMEM(phase_angles.shape, f32),
            pltpu.SMEM(pair_gate.shape, f32),
            pltpu.SMEM(slice_bits.shape, jnp.int32),
            pltpu.VMEM(flat.shape, f32),
        ]
        + [pltpu.VMEM((early, 2, m_size, low), f32)] * 4
        + [pltpu.VMEM((late, 2, m_size, low), f32)] * 4
        + [
            dma((2 * pieces,)), dma((5,)),
            dma((pieces,)), dma((pieces,)),
            dma((blocks,)), dma((blocks,)),
            dma((swaps,)), dma((swaps,)), dma((swaps,)), dma((swaps,)),
            dma((2 * blocks,)),
        ],
        compiler_params=pltpu.CompilerParams(
            collective_id=0, has_side_effects=True, vmem_limit_bytes=24 << 20
        ),
        name="evolve",
    )(*in_hbm)
    return out.reshape(amplitudes.shape)


def solution(mesh):
    spec = P(None, "grp", "swap", None, None, None, None, None)
    return jax.shard_map(
        functools.partial(local, mesh.shape["grp"], mesh.shape["swap"]),
        mesh=mesh,
        in_specs=(spec, P(), P(), P(), P(), P()),
        out_specs=spec,
        check_vma=False,
    )
```
